512 devices in a mesh: section: 8 (over y_lo, core), expert: 32 (over x, z), dp: 2 (over y_hi).
Axes of the slice: x: 4, y: 8 (y_hi: 2, y_lo: 4; y = y_hi * 4 + y_lo), z: 8, core: 2. Of those that a mesh axis runs over, the one named last changes fastest.
Arguments:
- tokens: bfloat16 [1024, 3072], P(('expert', 'dp')), may hold values from -6 to 6
- grad_out: bfloat16 [1024, 3072], P(('expert', 'dp')), may hold values from -6 to 6
- expert_ids: int32 [1024, 2], P(('expert', 'dp')), may hold values from 0 to 3, as said below
- gate_probs: float32 [1024, 2], P(('expert', 'dp')), may hold values from 0.1 to 0.9
- gate_weight: bfloat16 [3072, 32768], P('dp', ('expert', 'section')), may hold values from -0.109375 to 0.109375
- up_weight: bfloat16 [3072, 32768], P('dp', ('expert', 'section')), may hold values from -0.109375 to 0.109375
- down_weight: bfloat16 [3072, 32768], P('dp', ('expert', 'section')), may hold values from -0.0625 to 0.0625
Outputs:
- moe_out: bfloat16 [1024, 3072], P(('expert', 'dp'), 'section')
- grad_tokens: bfloat16 [1024, 3072], P(('expert', 'dp'), 'section')
- grad_gate: bfloat16 [3072, 32768], P('dp', ('expert', 'section'))
- grad_up: bfloat16 [3072, 32768], P('dp', ('expert', 'section'))
- grad_down: bfloat16 [3072, 32768], P('dp', ('expert', 'section'))
The draws below stay inside these ranges and needn't reach their ends.
Inputs may be any that keep to these rules, and one draw needn't show every extreme that they name: `expert_ids`: each token names two different experts. Among the 16 tokens of one index of expert and dp (aligned blocks of 16 rows) no expert is named more than 12 times. For each index of dp one expert, drawn from the seed, is named exactly 12 times in every block of that index; block b has dp index b % 2.
All inputs are finite; a program needn't handle non-finite values.
Results may differ from the reference program's by a relative error of at most 0.015.
Values may be sent and summed in bfloat16 or wider, within the bound.
A program may use at most 64 MiB of HBM per device.

```python
import jax
import jax.numpy as jnp
from jax import lax

D = 3072
EXP = 4
FF = 8192
TD = 16
CAP = 12
TOKENS = 1024
N_DP = 2


def draw_expert_ids(key, part):
    blocks = TOKENS // TD
    key_hot, key_offset, key_rank, key_flip = jax.random.split(key, 4)
    hot_expert = jax.random.randint(key_hot, (N_DP,), 0, EXP)
    offsets = jax.random.randint(key_offset, (blocks,), 0, EXP - 1)
    rank_keys = jax.random.split(key_rank, blocks)
    ranks = jax.vmap(lambda one_key: jax.random.permutation(one_key, TD))(rank_keys)
    flips = jax.random.randint(key_flip, (blocks, TD), 0, 2)
    block_hot = hot_expert[jnp.arange(blocks) % N_DP][:, None]
    cycle = (ranks + offsets[:, None]) % (EXP - 1)
    is_hot = ranks < CAP
    first_pick = jnp.where(is_hot, block_hot, (block_hot + 1 + (cycle + 1) % (EXP - 1)) % EXP)
    second_pick = jnp.where(is_hot, (block_hot + 1 + cycle) % EXP, (block_hot + 1 + (cycle + 2) % (EXP - 1)) % EXP)
    column_a = jnp.where(flips == 1, second_pick, first_pick)
    column_b = jnp.where(flips == 1, first_pick, second_pick)
    return jnp.stack([column_a, column_b], axis=-1).reshape(TOKENS, 2).astype(jnp.int32)


def block_scale(own_key, dims, shards, low, top_value):
    def one(axis_at, blocks):
        draws = jax.random.uniform(jax.random.fold_in(jax.random.fold_in(own_key, 6), axis_at), (blocks,), jnp.float32, low / len(shards), top_value / len(shards))
        return jnp.repeat(jnp.exp(draws), dims[axis_at] // blocks).reshape((-1,) + (1,) * (len(dims) - axis_at - 1))

    factor_of = one(*shards[0])
    for cut in shards[1:]:
        factor_of = factor_of * one(*cut)
    return factor_of


def centred(key, extent, spread, limit, pieces=(), held_as=jnp.bfloat16):
    loudness = block_scale(key, extent, pieces, -0.22, 0.18) if pieces else 1.0
    drawn = jax.random.normal(key, extent, jnp.float32) * spread * loudness
    return jnp.minimum(jnp.maximum(drawn, -limit), limit).astype(held_as)


def setup_inputs(seed: int = 0) -> dict:
    key_of = jax.random.split(jax.random.key(seed), 8)
    return {
        "tokens": centred(key_of[0], (TOKENS, D), 1.0, 6.0, ((0, 64),)),
        "grad_out": centred(key_of[1], (TOKENS, D), 1.0, 6.0, ((0, 64),)),
        "expert_ids": draw_expert_ids(jax.random.fold_in(key_of[7], 71), 0),
        "gate_probs": jnp.clip(0.1 + 0.79999997 * jax.random.uniform(key_of[3], (TOKENS, 2), jnp.float32) ** block_scale(key_of[3], (TOKENS, 2), ((0, 64),), -0.2, 0.2), 0.1, 0.9),
        "gate_weight": centred(key_of[4], (D, EXP * FF), D ** -0.5, 0.109375, ((0, 2), (1, 256))),
        "up_weight": centred(key_of[5], (D, EXP * FF), D ** -0.5, 0.109375, ((0, 2), (1, 256))),
        "down_weight": centred(key_of[6], (D, EXP * FF), FF ** -0.5, 0.0625, ((0, 2), (1, 256))),
    }


def half_sums(left, right):
    blocks = TOKENS // (TD * N_DP)
    left_halves = left.reshape(blocks, N_DP, TD, left.shape[1])
    right_halves = right.reshape(blocks, N_DP, TD, right.shape[1])
    summed = jnp.zeros((left.shape[1], right.shape[1]), jnp.float32)
    for half_index in range(N_DP):
        left_part = left_halves[:, half_index].reshape(-1, left.shape[1])
        right_part = right_halves[:, half_index].reshape(-1, right.shape[1])
        partial_value = jnp.dot(left_part.T, right_part, preferred_element_type=jnp.float32).astype(jnp.bfloat16)
        partial_value = lax.optimization_barrier(partial_value)
        summed = summed + partial_value.astype(jnp.float32)
    return summed.astype(jnp.bfloat16)


def reference(tokens, grad_out, expert_ids, gate_probs, gate_weight, up_weight, down_weight):
    moe_sum = jnp.zeros((TOKENS, D), jnp.float32)
    input_sum = jnp.zeros((TOKENS, D), jnp.float32)
    grads_gate = []
    grads_up = []
    grads_down = []
    for expert in range(EXP):
        gate_share = jnp.sum(jnp.where(expert_ids == expert, gate_probs, 0.0), axis=1)
        w_gate = gate_weight[:, expert * FF:(expert + 1) * FF]
        w_up = up_weight[:, expert * FF:(expert + 1) * FF]
        w_down = down_weight[:, expert * FF:(expert + 1) * FF]
        gate_pre = jnp.dot(tokens, w_gate, preferred_element_type=jnp.float32)
        up_pre = jnp.dot(tokens, w_up, preferred_element_type=jnp.float32)
        sigmoid_gate = jax.nn.sigmoid(gate_pre)
        silu_value = gate_pre * sigmoid_gate
        activation = (silu_value * up_pre).astype(jnp.bfloat16)
        expert_out = jnp.dot(activation, w_down.T, preferred_element_type=jnp.float32)
        moe_sum = moe_sum + gate_share[:, None] * expert_out
        scaled_grad = (gate_share[:, None] * grad_out.astype(jnp.float32)).astype(jnp.bfloat16)
        act_grad = jnp.dot(scaled_grad, w_down, preferred_element_type=jnp.float32)
        up_grad = (act_grad * silu_value).astype(jnp.bfloat16)
        gate_grad = (act_grad * up_pre * sigmoid_gate * (1.0 + gate_pre * (1.0 - sigmoid_gate))).astype(jnp.bfloat16)
        input_sum = input_sum + jnp.dot(gate_grad, w_gate.T, preferred_element_type=jnp.float32)
        input_sum = input_sum + jnp.dot(up_grad, w_up.T, preferred_element_type=jnp.float32)
        grads_gate.append(half_sums(tokens, gate_grad))
        grads_up.append(half_sums(tokens, up_grad))
        grads_down.append(half_sums(scaled_grad, activation))
    return (moe_sum.astype(jnp.bfloat16), input_sum.astype(jnp.bfloat16),
            jnp.concatenate(grads_gate, axis=1), jnp.concatenate(grads_up, axis=1),
            jnp.concatenate(grads_down, axis=1))
```

```python
import functools

import jax
import jax.numpy as jnp
from jax import lax
from jax.experimental import pallas as pl
from jax.experimental.pallas import tpu as pltpu
from jax.sharding import PartitionSpec as P

EXP = 4
CAP = 12
MESH = pl.DeviceIdType.MESH
F32 = jnp.float32
BF16 = jnp.bfloat16


def rows_dot(left, right):
    return lax.dot_general(left, right, (((0,), (0,)), ((), ())), preferred_element_type=F32)


def cols_dot(left, right):
    return lax.dot_general(left, right, (((1,), (1,)), ((), ())), preferred_element_type=F32)


class Ids:
    def __init__(self, nz, nx, nyl):
        self.count = 0
        half = nz // 2
        self.pair, self.share = self.take(1), self.take(1)
        self.to_expert = self.take(nx)
        self.up, self.down = self.take(half + 1), self.take(half + 1)
        self.twin = self.take(nz)
        self.hop_up, self.hop_down = self.take(nz), self.take(nz)
        self.end_up, self.end_down = self.take(nz), self.take(nz)
        self.out_twin = self.take(nz)
        self.sum_up, self.sum_down = self.take(half + 1), self.take(half + 1)
        self.to_source = self.take(nx)
        self.last = self.take(max(2 * (nyl // 2), nyl))

    def take(self, number):
        first = self.count
        self.count += number
        return first


def kernel(
    dims,
    tok, grd, expert_ids, gate_probs, w_gate, w_up, w_down,
    moe, gin, d_gate, d_up, d_down,
    staged, xs, share, rsend, gathered, weights,
    h_own, h_send, h_relay, h_other, hidden,
    o_own, o_send, o_twin, up_send, down_send, up_recv, down_recv,
    back_send, back_recv, last_send, last_recv, send_sem, recv_sem,
):
    nx, nz, nyl, feats, hid, td = dims
    half, nq = nz // 2, nyl // 2
    ny = 2 * nyl
    xh = nx // 2
    ids = Ids(nz, nx, nyl)
    section, place, yh = lax.axis_index("section"), lax.axis_index("expert"), lax.axis_index("dp")
    x, z = place // nz, lax.rem(place, nz)
    yl, c = section // 2, lax.rem(section, 2)
    y = yh * nyl + yl

    def at(x_to, z_to, y_to, c_to):
        return (lax.rem(y_to, nyl) * 2 + c_to, x_to * nz + z_to, y_to // nyl)

    def ring(value, size):
        return lax.rem(value + 2 * size, size)

    def copy(number, src, dst, to):
        return pltpu.make_async_remote_copy(
            src_ref=src, dst_ref=dst, send_sem=send_sem.at[number], recv_sem=recv_sem.at[number],
            device_id=to, device_id_type=MESH,
        )

    twin = at(x, z, y, 1 - c)
    above, below = at(x, ring(z + 1, nz), y, c), at(x, ring(z - 1, nz), y, c)
    hop = ny // 4
    north, south = at(x, z, ring(y + hop, ny), c), at(x, z, ring(y - hop, ny), c)
    pair = at(x, z, (1 - yh) * nyl + (nyl - 1 - yl), c)

    started = []

    def go(number, src, dst, to):
        one = copy(number, src, dst, to)
        one.start()
        started.append(one)

    def arrived(number, dst):
        copy(number, dst, dst, twin).wait_recv()

    barrier = pltpu.get_barrier_semaphore()
    for step in range(1, 2 * ny):
        other = ring(y * 2 + c + step, 2 * ny)
        pl.semaphore_signal(barrier, inc=1, device_id=at(x, z, other // 2, lax.rem(other, 2)), device_id_type=MESH)
    for step in range(1, nx):
        pl.semaphore_signal(barrier, inc=1, device_id=at(ring(x + step, nx), z, y, c), device_id_type=MESH)
    pl.semaphore_signal(barrier, inc=1, device_id=above, device_id_type=MESH)
    pl.semaphore_signal(barrier, inc=1, device_id=below, device_id_type=MESH)

    lane = lax.broadcasted_iota(jnp.int32, (td, 128), 1)
    gates = jnp.zeros((td, 128), F32)
    for k in range(2):
        gates = gates + jnp.where(expert_ids[:, k : k + 1] == lane, gate_probs[:, k : k + 1], 0.0)
    share[yh] = gates
    other_half = pl.ds(pl.multiple_of((1 - yh) * 2 * feats + c * feats, 128), feats)
    own_half = pl.ds(pl.multiple_of(yh * 2 * feats + c * feats, 128), feats)
    staged[0] = tok[:, other_half]
    staged[1] = grd[:, other_half]
    xs[yh, 0] = tok[:, own_half]
    xs[yh, 1] = grd[:, own_half]
    pl.semaphore_wait(barrier, 2 * ny - 1 + nx - 1 + 2)
    go(ids.pair, staged, xs.at[yh], pair)
    go(ids.share, share.at[yh], share.at[yh], pair)

    for h in range(2):
        part = slice(h * feats, (h + 1) * feats)
        weights[h, :, :hid] = w_gate[part, :]
        weights[h, :, hid : 2 * hid] = w_up[part, :]
        weights[h, :, 2 * hid :] = w_down[part, :]

    arrived(ids.share, share.at[1 - yh])
    arrived(ids.pair, xs.at[1 - yh])

    before = lax.broadcasted_iota(jnp.int32, (td, td), 1) < lax.broadcasted_iota(jnp.int32, (td, td), 0)
    before = jnp.where(before, 1.0, 0.0).astype(BF16)
    chosen = [jnp.where(share[d] > 0.0, 1.0, 0.0) for d in range(2)]
    rank = [jnp.dot(before, chosen[d].astype(BF16), preferred_element_type=F32) for d in range(2)]
    chosen4 = jnp.concatenate(chosen * 2, axis=0)
    rank4 = jnp.concatenate(
        [rank[0], rank[1] + CAP, rank[0] + 2 * CAP, rank[1] + 3 * CAP], axis=0
    )
    slot = lax.broadcasted_iota(jnp.int32, (4 * td, 4 * CAP), 1).astype(F32)

    def picks(e):
        same = jnp.where(rank4[:, e : e + 1] == slot, 1.0, 0.0)
        return (same * chosen4[:, e : e + 1]).astype(BF16)

    for e in range(nx):
        rows = [xs[0, 0], xs[1, 0]]
        for d in range(2):
            rows.append((share[d][:, e : e + 1] * xs[d, 1].astype(F32)).astype(BF16))
        rsend[e] = rows_dot(picks(e), jnp.concatenate(rows, axis=0)).astype(BF16)
    for step in range(1, nx):
        to = ring(x + step, nx)
        go(ids.to_expert + step, rsend.at[to], gathered.at[c, z, x], at(to, z, y, c))
    gathered[c, z, x] = rsend[x]
    for step in range(1, nx):
        arrived(ids.to_expert + step, gathered.at[c, z, ring(x - step, nx)])

    def gather_step(k):
        up_block, down_block = ring(z - k + 1, nz), ring(z + k - 1, nz)
        if k < half:
            up_part, down_part = gathered.at[c, up_block], gathered.at[c, down_block]
        else:
            up_part = gathered.at[c, up_block, pl.ds(0, xh)]
            down_part = gathered.at[c, down_block, pl.ds(xh, xh)]
        go(ids.up + k, up_part, up_part, above)
        go(ids.down + k, down_part, down_part, below)

    def gather_wait(k):
        up_block, down_block = ring(z - k, nz), ring(z + k, nz)
        if k < half:
            up_part, down_part = gathered.at[c, up_block], gathered.at[c, down_block]
        else:
            up_part = gathered.at[c, up_block, pl.ds(0, xh)]
            down_part = gathered.at[c, down_block, pl.ds(xh, xh)]
        arrived(ids.up + k, up_part)
        arrived(ids.down + k, down_part)

    def blocks(k):
        if k == 0:
            return [(z, 0)]
        if k == half:
            return [(ring(z + half, nz), nz - 1)]
        return [(ring(z - k, nz), 2 * k - 1), (ring(z + k, nz), 2 * k)]

    def each(k, body):
        if len(blocks(k)) == 1:
            body(*blocks(k)[0])
        else:
            def turn(i, carry):
                body(ring(z - k + 2 * k * i, nz), 2 * k - 1 + i)
                return carry
            lax.fori_loop(0, 2, turn, 0)

    def twin_share(k):
        for block, number in blocks(k):
            go(ids.twin + number, gathered.at[c, block], gathered.at[c, block], twin)

    slots = 4 * CAP

    def h_compute(k):
        def body(block, number):
            arrived(ids.twin + number, gathered.at[1 - c, block])
            total = jnp.dot(
                gathered[0, block].reshape(nx * slots, feats), weights[0], preferred_element_type=F32
            ) + jnp.dot(
                gathered[1, block].reshape(nx * slots, feats), weights[1], preferred_element_type=F32
            )
            total = total.reshape(nx, slots, 3 * hid)
            value = jnp.concatenate(
                [total[:, : slots // 2, : 2 * hid], total[:, slots // 2 :, 2 * hid :]], axis=2
            ).reshape(nx * slots // 2, 3 * hid)
            h_own[block] = value
            h_send[block] = value.reshape(2, nx * slots // 4, 3 * hid).astype(BF16)
        each(k, body)
        for block, number in blocks(k):
            go(ids.hop_up + number, h_send.at[block, 0], h_relay.at[block, 0], north)
            go(ids.hop_down + number, h_send.at[block, 1], h_relay.at[block, 1], south)

    def relay(k):
        for block, number in blocks(k):
            arrived(ids.hop_up + number, h_relay.at[block, 0])
            go(ids.end_up + number, h_relay.at[block, 0], h_other.at[block, 0], north)
            arrived(ids.hop_down + number, h_relay.at[block, 1])
            go(ids.end_down + number, h_relay.at[block, 1], h_other.at[block, 1], south)

    def outputs(k):
        def body(block, number):
            arrived(ids.end_up + number, h_other.at[block, 0])
            arrived(ids.end_down + number, h_other.at[block, 1])
            full = h_own[block] + h_other[block].reshape(nx * slots // 2, 3 * hid).astype(F32)
            gate_pre, up_pre, act_grad = full[:, :hid], full[:, hid : 2 * hid], full[:, 2 * hid :]
            sigmoid_gate = jax.nn.sigmoid(gate_pre)
            silu = gate_pre * sigmoid_gate
            activation = silu * up_pre
            up_grad = act_grad * silu
            gate_grad = act_grad * up_pre * sigmoid_gate * (1.0 + gate_pre * (1.0 - sigmoid_gate))
            zero = jnp.zeros_like(activation)
            first = jnp.concatenate([gate_grad, up_grad, zero], axis=1).reshape(nx, slots // 2, 3 * hid)
            second = jnp.concatenate([zero, zero, activation], axis=1).reshape(nx, slots // 2, 3 * hid)
            value = jnp.concatenate([first, second], axis=1).reshape(nx * slots, 3 * hid).astype(BF16)
            hidden[block] = value
            o_own[block] = cols_dot(value, weights[c]).reshape(nx, slots, feats)
            o_send[block] = cols_dot(value, weights[1 - c]).reshape(nx, slots, feats).astype(BF16)
        each(k, body)
        for block, number in blocks(k):
            go(ids.out_twin + number, o_send.at[block], o_twin.at[block], twin)

    gather_step(1)
    twin_share(0)
    for k in range(1, half + 1):
        gather_wait(k)
        if k < half:
            gather_step(k + 1)
        twin_share(k)
        h_compute(k - 1)
        if k >= 2:
            relay(k - 2)
        if k >= 3:
            outputs(k - 3)
    h_compute(half)
    relay(half - 1)
    outputs(half - 2)
    relay(half)
    outputs(half - 1)
    outputs(half)

    tile = min(feats, 256)
    tiles = 2 * (feats // tile)

    def weight_grads(first, last):
        def turn(t, carry):
            h, j = t // (feats // tile), lax.rem(t, feats // tile)
            left = gathered[h, :, :, :, pl.ds(pl.multiple_of(j * tile, 128), tile)]
            value = rows_dot(
                left.reshape(nz * nx * slots, tile), hidden[...].reshape(nz * nx * slots, 3 * hid)
            ).astype(BF16)
            rows = pl.ds(pl.multiple_of(t * tile, 128), tile)
            d_gate[rows, :] = value[:, :hid]
            d_up[rows, :] = value[:, hid : 2 * hid]
            d_down[rows, :] = value[:, 2 * hid :]
            return carry
        lax.fori_loop(first, last, turn, 0)

    def own_sum(block):
        return o_own[block] + o_twin[block].astype(F32)

    def out_arrived(k):
        for block, number in blocks(k):
            arrived(ids.out_twin + number, o_twin.at[block])

    out_arrived(half)
    far = ring(z + half, nz)
    value = own_sum(far).astype(BF16)
    up_send[1, :xh] = value[:xh]
    down_send[1, xh:] = value[xh:]
    go(ids.sum_up + 1, up_send.at[1, pl.ds(0, xh)], up_recv.at[1, pl.ds(0, xh)], above)
    go(ids.sum_down + 1, down_send.at[1, pl.ds(xh, xh)], down_recv.at[1, pl.ds(xh, xh)], below)
    done = 0
    for step in range(2, half + 1):
        until = (tiles * (step - 1)) // (half - 1)
        weight_grads(done, until)
        done = until
        away = half + 1 - step
        out_arrived(away)
        if step == 2:
            up_send[step] = own_sum(ring(z + away, nz)).astype(BF16)
            down_send[step] = own_sum(ring(z - away, nz)).astype(BF16)
            arrived(ids.sum_up + 1, up_recv.at[1, pl.ds(0, xh)])
            part = own_sum(ring(z + away, nz))[:xh] + up_recv[1, :xh].astype(F32)
            up_send[step, :xh] = part.astype(BF16)
            go(ids.sum_up + step, up_send.at[step], up_recv.at[step], above)
            arrived(ids.sum_down + 1, down_recv.at[1, pl.ds(xh, xh)])
            part = own_sum(ring(z - away, nz))[xh:] + down_recv[1, xh:].astype(F32)
            down_send[step, xh:] = part.astype(BF16)
            go(ids.sum_down + step, down_send.at[step], down_recv.at[step], below)
        else:
            arrived(ids.sum_up + step - 1, up_recv.at[step - 1])
            value = own_sum(ring(z + away, nz)) + up_recv[step - 1].astype(F32)
            up_send[step] = value.astype(BF16)
            go(ids.sum_up + step, up_send.at[step], up_recv.at[step], above)
            arrived(ids.sum_down + step - 1, down_recv.at[step - 1])
            value = own_sum(ring(z - away, nz)) + down_recv[step - 1].astype(F32)
            down_send[step] = value.astype(BF16)
            go(ids.sum_down + step, down_send.at[step], down_recv.at[step], below)
    out_arrived(0)
    arrived(ids.sum_up + half, up_recv.at[half])
    arrived(ids.sum_down + half, down_recv.at[half])
    value = own_sum(z) + up_recv[half].astype(F32) + down_recv[half].astype(F32)
    back_send[...] = value.astype(BF16)
    for step in range(1, nx):
        to = ring(x + step, nx)
        go(ids.to_source + step, back_send.at[to], back_recv.at[x], at(to, z, y, c))
    back_recv[x] = back_send[x]
    for step in range(1, nx):
        source = ring(x - step, nx)
        arrived(ids.to_source + step, back_recv.at[source])

    combined = jnp.zeros((4 * td, feats), F32)
    ones = jnp.ones((td, 1), F32)
    for e in range(nx):
        scale = jnp.concatenate([ones, ones, share[0][:, e : e + 1], share[1][:, e : e + 1]], axis=0)
        picked = jnp.dot(picks(e), back_recv[e], preferred_element_type=F32)
        combined = combined + scale * picked
    combined = combined.astype(BF16)
    width = feats // nq
    for d in range(2):
        for q in range(nq):
            columns = slice(q * width, (q + 1) * width)
            last_send[d, q, :td] = combined[d * td : (d + 1) * td, columns]
            last_send[d, q, td:] = combined[(2 + d) * td : (3 + d) * td, columns]
    copies = []
    for d in range(2):
        for q in range(nq):
            owner = yh * nyl + c * nq + q
            y_to, c_to = d * nyl + owner // 2, lax.rem(owner, 2)
            mine = jnp.logical_and(y_to == y, c_to == c)
            one = pltpu.make_async_remote_copy(
                src_ref=last_send.at[d, q], dst_ref=last_recv.at[yl],
                send_sem=send_sem.at[ids.last + d * nq + q], recv_sem=recv_sem.at[ids.last + yl],
                device_id=at(x, z, y_to, c_to), device_id_type=MESH,
            )
            copies.append((mine, one))

            @pl.when(mine)
            def _():
                last_recv[yl] = last_send[d, q]

            @pl.when(jnp.logical_not(mine))
            def _():
                one.start()

    from_yh, from_c = section // nyl, lax.rem(section, nyl) // nq
    for yl_from in range(nyl):
        mine = jnp.logical_and(from_yh * nyl + yl_from == y, from_c == c)

        @pl.when(jnp.logical_not(mine))
        def _():
            arrived(ids.last + yl_from, last_recv.at[yl_from])

    total = last_recv[0].astype(F32)
    for yl_from in range(1, nyl):
        total = total + last_recv[yl_from].astype(F32)
    gin[...] = total[:td].astype(BF16)
    moe[...] = total[td:].astype(BF16)

    for one in started:
        one.wait_send()
    for mine, one in copies:

        @pl.when(jnp.logical_not(mine))
        def _():
            one.wait_send()


def local(nyl, tokens, grad_out, expert_ids, gate_probs, gate_weight, up_weight, down_weight):
    td, width = tokens.shape
    hid = gate_weight.shape[1]
    nx = EXP
    nz = lax.axis_size("expert") // nx
    feats = width // 4
    nq = nyl // 2
    slots = 4 * CAP
    half = nz // 2
    count = Ids(nz, nx, nyl).count
    vmem = pl.BlockSpec(memory_space=pltpu.VMEM)
    out_token = jax.ShapeDtypeStruct((td, width // (2 * nyl)), BF16)
    out_weight = jax.ShapeDtypeStruct(gate_weight.shape, BF16)
    exchange = pltpu.VMEM((nz, 2, nx * slots // 4, 3 * hid), BF16)
    ring_slots = pltpu.VMEM((half + 1, nx, slots, feats), BF16)
    return pl.pallas_call(
        functools.partial(kernel, (nx, nz, nyl, feats, hid, td)),
        out_shape=(out_token, out_token, out_weight, out_weight, out_weight),
        in_specs=[vmem] * 7,
        out_specs=(vmem,) * 5,
        scratch_shapes=[
            pltpu.VMEM((2, td, feats), BF16),
            pltpu.VMEM((2, 2, td, feats), BF16),
            pltpu.VMEM((2, td, 128), F32),
            pltpu.VMEM((nx, slots, feats), BF16),
            pltpu.VMEM((2, nz, nx, slots, feats), BF16),
            pltpu.VMEM((2, feats, 3 * hid), BF16),
            pltpu.VMEM((nz, nx * slots // 2, 3 * hid), F32),
            exchange,
            exchange,
            exchange,
            pltpu.VMEM((nz, nx * slots, 3 * hid), BF16),
            pltpu.VMEM((nz, nx, slots, feats), F32),
            pltpu.VMEM((nz, nx, slots, feats), BF16),
            pltpu.VMEM((nz, nx, slots, feats), BF16),
            ring_slots,
            ring_slots,
            ring_slots,
            ring_slots,
            pltpu.VMEM((nx, slots, feats), BF16),
            pltpu.VMEM((nx, slots, feats), BF16),
            pltpu.VMEM((2, nq, 2 * td, feats // nq), BF16),
            pltpu.VMEM((nyl, 2 * td, feats // nq), BF16),
            pltpu.SemaphoreType.DMA((count,)),
            pltpu.SemaphoreType.DMA((count,)),
        ],
        compiler_params=pltpu.CompilerParams(
            collective_id=0, has_side_effects=True, vmem_limit_bytes=60 * 1024 * 1024
        ),
        name="moe_layer",
    )(tokens, grad_out, expert_ids, gate_probs, gate_weight, up_weight, down_weight)


def solution(mesh):
    return jax.shard_map(
        functools.partial(local, mesh.shape["section"] // 2),
        mesh=mesh,
        in_specs=(
            P(("expert", "dp"), None),
            P(("expert", "dp"), None),
            P(("expert", "dp"), None),
            P(("expert", "dp"), None),
            P("dp", ("expert", "section")),
            P("dp", ("expert", "section")),
            P("dp", ("expert", "section")),
        ),
        out_specs=(
            P(("expert", "dp"), "section"),
            P(("expert", "dp"), "section"),
            P("dp", ("expert", "section")),
            P("dp", ("expert", "section")),
            P("dp", ("expert", "section")),
        ),
        check_vma=False,
    )
```

```python
import functools

import jax
import jax.numpy as jnp
from jax import lax
from jax.experimental import pallas as pl
from jax.experimental.pallas import tpu as pltpu
from jax.sharding import PartitionSpec as P

EXP = 4
CAP = 12
MESH = pl.DeviceIdType.MESH
F32 = jnp.float32
BF16 = jnp.bfloat16


def rows_dot(left, right):
    return lax.dot_general(left, right, (((0,), (0,)), ((), ())), preferred_element_type=F32)


def cols_dot(left, right):
    return lax.dot_general(left, right, (((1,), (1,)), ((), ())), preferred_element_type=F32)


LAG = 2


def kernel(
    dims,
    tok, grd, expert_ids, gate_probs, w_gate, w_up, w_down,
    moe, gin, d_gate, d_up, d_down,
    staged, xs, share, picks, scales, rsend, gathered, weights,
    h_own, h_send, h_other, hidden,
    o_own, o_send, o_twin, up_send, down_send, up_recv, down_recv,
    back_send, back_recv, last_send, last_recv, grads, send_sem, recv_sem, load_sem,
):
    nx, nz, nyl, feats, hid, td = dims
    half, nq = nz // 2, nyl // 2
    ny = 2 * nyl
    slots = 4 * CAP
    near = slots // 2
    section, place, yh = lax.axis_index("section"), lax.axis_index("expert"), lax.axis_index("dp")
    x, z = place // nz, lax.rem(place, nz)
    yl, c = section // 2, lax.rem(section, 2)
    y = yh * nyl + yl

    def at(x_to, z_to, y_to, c_to):
        return (lax.rem(y_to, nyl) * 2 + c_to, x_to * nz + z_to, y_to // nyl)

    def ring(value, size):
        return lax.rem(value + 2 * size, size)

    twin = at(x, z, y, 1 - c)
    above, below = at(x, ring(z + 1, nz), y, c), at(x, ring(z - 1, nz), y, c)
    across = at(x, z, ring(y + nyl, ny), c)
    pair = at(x, z, (1 - yh) * nyl + (nyl - 1 - yl), c)

    numbers = {}
    started = []

    def number_of(name):
        return numbers.setdefault(name, len(numbers))

    def copy(name, src, dst, to):
        number = number_of(name)
        return pltpu.make_async_remote_copy(
            src_ref=src, dst_ref=dst, send_sem=send_sem.at[number], recv_sem=recv_sem.at[number],
            device_id=to, device_id_type=MESH,
        )

    def go(name, src, dst, to):
        one = copy(name, src, dst, to)
        one.start()
        started.append(one)

    def arrived(name, dst):
        copy(name, dst, dst, twin).wait_recv()

    loads = []
    for h in range(2):
        for i, ref in enumerate((w_gate, w_up, w_down)):
            load = pltpu.make_async_copy(
                ref.at[pl.ds(h * feats, feats), :], weights.at[h, :, pl.ds(i * hid, hid)], load_sem.at[3 * h + i]
            )
            load.start()
            loads.append(load)
    barrier = pltpu.get_barrier_semaphore()
    for step in range(1, 2 * ny):
        other = ring(y * 2 + c + step, 2 * ny)
        pl.semaphore_signal(barrier, inc=1, device_id=at(x, z, other // 2, lax.rem(other, 2)), device_id_type=MESH)
    for step in range(1, nx):
        pl.semaphore_signal(barrier, inc=1, device_id=at(ring(x + step, nx), z, y, c), device_id_type=MESH)
    pl.semaphore_signal(barrier, inc=1, device_id=above, device_id_type=MESH)
    pl.semaphore_signal(barrier, inc=1, device_id=below, device_id_type=MESH)

    row = lax.broadcasted_iota(jnp.int32, (128, td), 0)
    gates = jnp.zeros((128, td), F32)
    for k in range(2):
        gates = gates + jnp.where(expert_ids[k : k + 1, :] == row, gate_probs[k : k + 1, :], 0.0)
    share[yh] = gates.T
    other_half = pl.ds(pl.multiple_of((1 - yh) * 2 * feats + c * feats, 128), feats)
    own_half = pl.ds(pl.multiple_of(yh * 2 * feats + c * feats, 128), feats)
    staged[0] = tok[:, other_half]
    staged[1] = grd[:, other_half]
    xs[yh, 0] = tok[:, own_half]
    xs[yh, 1] = grd[:, own_half]
    pl.semaphore_wait(barrier, 2 * ny - 1 + nx - 1 + 2)
    go("share", share.at[yh], share.at[yh], pair)
    go("pair", staged, xs.at[yh], pair)

    before = lax.broadcasted_iota(jnp.int32, (td, td), 1) < lax.broadcasted_iota(jnp.int32, (td, td), 0)
    before = jnp.where(before, 1.0, 0.0).astype(BF16)
    slot = lax.broadcasted_iota(jnp.int32, (2 * td, slots), 1).astype(F32)
    shift = jnp.where(lax.broadcasted_iota(jnp.int32, (2 * td, 1), 0) < td, 0.0, 2.0 * CAP)

    def tables(d):
        gate = share[d]
        first = (d * CAP).astype(F32)
        chosen = jnp.where(gate > 0.0, 1.0, 0.0)
        rank = jnp.dot(before, chosen.astype(BF16), preferred_element_type=F32)
        ones = jnp.ones((td, 128), F32)
        for e in range(nx):
            rank_e, chosen_e = rank[:, e : e + 1], chosen[:, e : e + 1]
            rank2 = jnp.concatenate([rank_e, rank_e], axis=0) + (shift + first)
            chosen2 = jnp.concatenate([chosen_e, chosen_e], axis=0)
            picks[e, d] = (jnp.where(rank2 == slot, 1.0, 0.0) * chosen2).astype(BF16)
            gate_e = jnp.broadcast_to(gate[:, e : e + 1], (td, 128))
            scales[e, d] = jnp.concatenate([ones, gate_e], axis=0)

    tables(yh)
    arrived("share", share.at[1 - yh])
    tables(1 - yh)
    arrived("pair", xs.at[1 - yh])
    stacked = xs[...].reshape(4 * td, feats).astype(F32)

    def pick_for(e):
        scale = scales[e].reshape(4 * td, 128)[:, :1]
        rows = (scale * stacked).astype(BF16)
        return rows_dot(picks[e].reshape(4 * td, slots), rows).astype(BF16)

    def first_of(k):
        return 0 if k == 0 else 2 * k - 1

    def size_of(k):
        return 1 if k in (0, half) else 2

    def span(k):
        return pl.ds(first_of(k), size_of(k))

    def landing(k, side):
        return nz - 1 if k == half else 2 * k - 1 + side

    def sends(t, k, p, side):
        return k < half or p == side

    width = feats // 2

    def column(i):
        return slice(i * width, (i + 1) * width)

    def columns_of(ref, i):
        return ref.at[:, pl.ds(i * width, width)]

    def gather_send(t, k, p):
        for i in range(2):
            for side, to in ((0, above), (1, below)):
                if sends(t, k, p, side):
                    part = columns_of(gathered.at[c, t, 0, p], i)
                    go(("gather", t, k, p, i, side), part, columns_of(gathered.at[c, t, landing(k, side), p], i), to)

    def gather_take(t, k):
        for p in range(2):
            for i in range(2):
                for side, to in ((0, above), (1, below)):
                    if sends(t, k, p, side):
                        part = columns_of(gathered.at[c, t, landing(k, side), p], i)
                        arrived(("gather", t, k, p, i, side), part)
                        if k < half and sends(t, k + 1, p, side):
                            there = columns_of(gathered.at[c, t, landing(k + 1, side), p], i)
                            go(("gather", t, k + 1, p, i, side), part, there, to)
        twin_share(t, k)

    def twin_share(t, k):
        part = gathered.at[c, t, span(k)]
        go(("twin", t, k), part, part, twin)

    def compute_h(t, k):
        arrived(("twin", t, k), gathered.at[1 - c, t, span(k)])
        n, first = size_of(k), first_of(k)
        total = jnp.dot(
            gathered[0, t, first : first + n].reshape(n * 2 * slots, feats), weights[0], preferred_element_type=F32
        ) + jnp.dot(
            gathered[1, t, first : first + n].reshape(n * 2 * slots, feats), weights[1], preferred_element_type=F32
        )
        total = total.reshape(n * 2, slots, 3 * hid)
        value = jnp.concatenate([total[:, :near, : 2 * hid], total[:, near:, 2 * hid :]], axis=2)
        value = value.reshape(n, slots, 3 * hid)
        h_own[t, first : first + n] = value
        h_send[t, first : first + n] = value.astype(BF16)
        for b in range(first, first + n):
            go(("swap", t, b), h_send.at[t, b], h_other.at[t, b], across)

    def outputs(t, k):
        n, first = size_of(k), first_of(k)
        for b in range(first, first + n):
            arrived(("swap", t, b), h_other.at[t, b])
        full = h_own[t, first : first + n] + h_other[t, first : first + n].astype(F32)
        full = full.reshape(n * slots, 3 * hid)
        gate_pre, up_pre, act_grad = full[:, :hid], full[:, hid : 2 * hid], full[:, 2 * hid :]
        sigmoid_gate = jax.nn.sigmoid(gate_pre)
        silu = gate_pre * sigmoid_gate
        activation = silu * up_pre
        up_grad = act_grad * silu
        gate_grad = act_grad * up_pre * sigmoid_gate * (1.0 + gate_pre * (1.0 - sigmoid_gate))
        zero = jnp.zeros_like(activation)
        upper = jnp.concatenate([gate_grad, up_grad, zero], axis=1).reshape(n * 2, near, 3 * hid)
        lower = jnp.concatenate([zero, zero, activation], axis=1).reshape(n * 2, near, 3 * hid)
        value = jnp.concatenate([upper, lower], axis=1).reshape(n * 2 * slots, 3 * hid).astype(BF16)
        hidden[t, first : first + n] = value.reshape(n, 2, slots, 3 * hid)
        o_send[t, first : first + n] = cols_dot(value, weights[1 - c]).astype(BF16).reshape(n, 2, slots, feats)
        go(("out", t, k), o_send.at[t, span(k)], o_twin.at[t, span(k)], twin)
        o_own[t, first : first + n] = cols_dot(value, weights[c]).reshape(n, 2, slots, feats)

    def own_sum(t, b, p, i):
        return o_own[t, b, p, :, column(i)] + o_twin[t, b, p, :, column(i)].astype(F32)

    def sum_step(t, step):
        away = half + 1 - step
        arrived(("out", t, away), o_twin.at[t, span(away)])
        parts = [(p, i, side) for p in range(2) for i in range(2) for side in range(2)]
        if step == 1:
            parts = [part for part in parts if part[0] == part[2]]
        if step == 2:
            parts.sort(key=lambda part: part[0] == part[2])
        for p, i, side in parts:
            to, out_ref, in_ref = ((above, up_send, up_recv), (below, down_send, down_recv))[side]
            value = own_sum(t, nz - 1 if step == 1 else 2 * away - side, p, i)
            if step > 2 or (step == 2 and p == side):
                arrived(("sum", t, step - 1, p, i, side), columns_of(in_ref.at[t, step - 1, p], i))
                value = value + in_ref[t, step - 1, p, :, column(i)].astype(F32)
            out_ref[t, step, p, :, column(i)] = value.astype(BF16)
            go(
                ("sum", t, step, p, i, side),
                columns_of(out_ref.at[t, step, p], i), columns_of(in_ref.at[t, step, p], i), to,
            )

    def sum_end(t):
        arrived(("out", t, 0), o_twin.at[t, span(0)])
        for p in range(2):
            j = 2 * t + p
            for i in range(2):
                for side, in_ref in ((0, up_recv), (1, down_recv)):
                    arrived(("sum", t, half, p, i, side), columns_of(in_ref.at[t, half, p], i))
                value = own_sum(t, 0, p, i) + up_recv[t, half, p, :, column(i)].astype(F32)
                value = value + down_recv[t, half, p, :, column(i)].astype(F32)
                if j:
                    back_send[t, p, :, column(i)] = value.astype(BF16)
                else:
                    back_recv[0, :, column(i)] = value.astype(BF16)
            if j:
                go(("back", j), back_send.at[t, p], back_recv.at[j], at(ring(x - j, nx), z, y, c))

    def combine(t):
        total = jnp.zeros((4 * td, feats), F32)
        for j in (2 * t, 2 * t + 1):
            if j:
                arrived(("back", j), back_recv.at[j])
            e = ring(x + j, nx)
            scale = scales[e].reshape(4 * td, 128)[:, :1]
            total = total + scale * jnp.dot(
                picks[e].reshape(4 * td, slots), back_recv[j], preferred_element_type=F32
            )
        return total

    tile = min(feats, 256)
    tiles = 2 * (feats // tile)

    def weight_grads(first, last):
        def turn(i, carry):
            h, j = i // (feats // tile), lax.rem(i, feats // tile)
            left = gathered[h, :, :, :, :, pl.ds(pl.multiple_of(j * tile, 128), tile)]
            value = rows_dot(
                left.reshape(nz * nx * slots, tile), hidden[...].reshape(nz * nx * slots, 3 * hid)
            ).astype(BF16)
            rows = pl.ds(pl.multiple_of(i * tile, 128), tile)
            for part in range(3):
                grads[part, rows, :] = value[:, part * hid : (part + 1) * hid]
            return carry
        lax.fori_loop(first, last, turn, 0)

    gathered[c, 0, 0, 0] = pick_for(x)
    gather_send(0, 1, 0)
    for j in range(1, nx):
        e = ring(x + j, nx)
        rsend[j] = pick_for(e)
        go(("expert", j), rsend.at[j], gathered.at[c, j // 2, 0, j % 2], at(e, z, y, c))
    arrived(("expert", 1), gathered.at[c, 0, 0, 1])
    gather_send(0, 1, 1)
    twin_share(0, 0)

    def valid(k):
        return 0 <= k <= half

    for turn in range(1, half + LAG + 1):
        if turn <= half:
            gather_take(0, turn)
        if turn == LAG:
            for p in range(2):
                arrived(("expert", 2 + p), gathered.at[c, 1, 0, p])
                gather_send(1, 1, p)
            twin_share(1, 0)
        if turn == 1:
            for load in loads:
                load.wait()
        if valid(turn - 1):
            compute_h(0, turn - 1)
        if turn > LAG:
            gather_take(1, turn - LAG)
        if valid(turn - LAG - 1):
            compute_h(1, turn - LAG - 1)
        if valid(turn - 3):
            outputs(0, turn - 3)
        if valid(turn - LAG - 3):
            outputs(1, turn - LAG - 3)
    compute_h(1, half)
    for k in range(half + LAG - 2, half + 1):
        outputs(0, k)
    sum_step(0, 1)
    for step in range(2, half):
        outputs(1, half + step - 4)
        sum_step(0, step)
    for k in range(2 * half - 4, half + 1):
        outputs(1, k)
    sum_step(1, 1)
    weight_grads(0, tiles // 6)
    sum_step(0, half)
    weight_grads(tiles // 6, tiles // 3)
    sum_step(1, 2)
    weight_grads(tiles // 3, tiles // 2)
    sum_end(0)
    for step in range(3, half):
        sum_step(1, step)
    weight_grads(tiles // 2, tiles)
    results = []
    for i, ref in enumerate((d_gate, d_up, d_down)):
        result = pltpu.make_async_copy(grads.at[i], ref, load_sem.at[6 + i])
        result.start()
        results.append(result)
    if half > 2:
        sum_step(1, half)
    combined = combine(0)
    sum_end(1)
    combined = (combined + combine(1)).astype(BF16)
    share_of = feats // nq
    for d in range(2):
        for q in range(nq):
            last_send[d, q] = combined[2 * d * td : 2 * (d + 1) * td, q * share_of : (q + 1) * share_of]
    copies = []
    senders = [number_of(("last", i)) for i in range(2 * nq)]
    takers = [number_of(("take", i)) for i in range(nyl)]
    for d in range(2):
        for q in range(nq):
            owner = yh * nyl + c * nq + q
            y_to, c_to = d * nyl + owner // 2, lax.rem(owner, 2)
            mine = jnp.logical_and(y_to == y, c_to == c)
            one = pltpu.make_async_remote_copy(
                src_ref=last_send.at[d, q], dst_ref=last_recv.at[yl],
                send_sem=send_sem.at[senders[d * nq + q]], recv_sem=recv_sem.at[takers[0] + yl],
                device_id=at(x, z, y_to, c_to), device_id_type=MESH,
            )
            copies.append((mine, one))

            @pl.when(mine)
            def _():
                last_recv[yl] = last_send[d, q]

            @pl.when(jnp.logical_not(mine))
            def _():
                one.start()

    from_yh, from_c = section // nyl, lax.rem(section, nyl) // nq
    for yl_from in range(nyl):
        mine = jnp.logical_and(from_yh * nyl + yl_from == y, from_c == c)

        @pl.when(jnp.logical_not(mine))
        def _():
            arrived(("take", yl_from), last_recv.at[yl_from])

    total = last_recv[0].astype(F32)
    for yl_from in range(1, nyl):
        total = total + last_recv[yl_from].astype(F32)
    gin[...] = total[:td].astype(BF16)
    moe[...] = total[td:].astype(BF16)

    for one in results:
        one.wait()
    for one in started:
        one.wait_send()
    for mine, one in copies:

        @pl.when(jnp.logical_not(mine))
        def _():
            one.wait_send()


SEMAPHORES = 192


def local(nyl, tokens, grad_out, expert_ids, gate_probs, gate_weight, up_weight, down_weight):
    td, width = tokens.shape
    hid = gate_weight.shape[1]
    nx = EXP
    nz = lax.axis_size("expert") // nx
    feats = width // 4
    nq = nyl // 2
    slots = 4 * CAP
    half = nz // 2
    vmem = pl.BlockSpec(memory_space=pltpu.VMEM)
    out_token = jax.ShapeDtypeStruct((td, width // (2 * nyl)), BF16)
    out_weight = jax.ShapeDtypeStruct(gate_weight.shape, BF16)
    exchange = pltpu.VMEM((2, nz, slots, 3 * hid), BF16)
    outs = pltpu.VMEM((2, nz, 2, slots, feats), BF16)
    ring_slots = pltpu.VMEM((2, half + 1, 2, slots, feats), BF16)
    anywhere = pl.BlockSpec(memory_space=pl.ANY)
    results = pl.pallas_call(
        functools.partial(kernel, (nx, nz, nyl, feats, hid, td)),
        out_shape=(out_token, out_token, out_weight, out_weight, out_weight),
        in_specs=[vmem] * 4 + [anywhere] * 3,
        out_specs=(vmem,) * 2 + (anywhere,) * 3,
        scratch_shapes=[
            pltpu.VMEM((2, td, feats), BF16),
            pltpu.VMEM((2, 2, td, feats), BF16),
            pltpu.VMEM((2, td, 128), F32),
            pltpu.VMEM((nx, 2, 2 * td, slots), BF16),
            pltpu.VMEM((nx, 2, 2 * td, 128), F32),
            pltpu.VMEM((nx, slots, feats), BF16),
            pltpu.VMEM((2, 2, nz, 2, slots, feats), BF16),
            pltpu.VMEM((2, feats, 3 * hid), BF16),
            pltpu.VMEM((2, nz, slots, 3 * hid), F32),
            exchange,
            exchange,
            pltpu.VMEM((2, nz, 2, slots, 3 * hid), BF16),
            pltpu.VMEM((2, nz, 2, slots, feats), F32),
            outs,
            outs,
            ring_slots,
            ring_slots,
            ring_slots,
            ring_slots,
            pltpu.VMEM((2, 2, slots, feats), BF16),
            pltpu.VMEM((nx, slots, feats), BF16),
            pltpu.VMEM((2, nq, 2 * td, feats // nq), BF16),
            pltpu.VMEM((nyl, 2 * td, feats // nq), BF16),
            pltpu.VMEM((3, 2 * feats, hid), BF16),
            pltpu.SemaphoreType.DMA((SEMAPHORES,)),
            pltpu.SemaphoreType.DMA((SEMAPHORES,)),
            pltpu.SemaphoreType.DMA((9,)),
        ],
        compiler_params=pltpu.CompilerParams(
            collective_id=0, has_side_effects=True, vmem_limit_bytes=60 * 1024 * 1024
        ),
        name="moe_layer",
    )(tokens, grad_out, expert_ids.T, gate_probs.T, gate_weight, up_weight, down_weight)
    return pl.pallas_call(
        hand_on,
        out_shape=tuple(jax.ShapeDtypeStruct(one.shape, one.dtype) for one in results),
        in_specs=[vmem] * 5,
        out_specs=(vmem,) * 5,
        name="hand_on",
    )(*results)


def hand_on(*refs):
    for source, target in zip(refs[:5], refs[5:]):
        target[...] = source[...]


def solution(mesh):
    return jax.shard_map(
        functools.partial(local, mesh.shape["section"] // 2),
        mesh=mesh,
        in_specs=(
            P(("expert", "dp"), None),
            P(("expert", "dp"), None),
            P(("expert", "dp"), None),
            P(("expert", "dp"), None),
            P("dp", ("expert", "section")),
            P("dp", ("expert", "section")),
            P("dp", ("expert", "section")),
        ),
        out_specs=(
            P(("expert", "dp"), "section"),
            P(("expert", "dp"), "section"),
            P("dp", ("expert", "section")),
            P("dp", ("expert", "section")),
            P("dp", ("expert", "section")),
        ),
        check_vma=False,
    )
```

```python
import functools

import jax
import jax.numpy as jnp
from jax import lax
from jax.experimental import pallas as pl
from jax.experimental.pallas import tpu as pltpu
from jax.sharding import PartitionSpec as P

EXP = 4
CAP = 12
MESH = pl.DeviceIdType.MESH
F32 = jnp.float32
BF16 = jnp.bfloat16


def rows_dot(left, right):
    return lax.dot_general(left, right, (((0,), (0,)), ((), ())), preferred_element_type=F32)


def cols_dot(left, right):
    return lax.dot_general(left, right, (((1,), (1,)), ((), ())), preferred_element_type=F32)


LAG = 2


def kernel(
    dims,
    tok, grd, expert_ids, gate_probs, w_gate, w_up, w_down,
    moe, gin, d_gate, d_up, d_down,
    staged, xs, share, picks, scales, rsend, gathered, weights,
    h_own, h_send, h_other, hidden,
    o_own, o_send, o_twin, up_send, down_send, up_recv, down_recv,
    back_send, back_recv, last_send, last_recv, grads, send_sem, recv_sem, load_sem,
):
    nx, nz, nyl, feats, hid, td = dims
    half, nq = nz // 2, nyl // 2
    ny = 2 * nyl
    slots = 4 * CAP
    near = slots // 2
    section, place, yh = lax.axis_index("section"), lax.axis_index("expert"), lax.axis_index("dp")
    x, z = place // nz, lax.rem(place, nz)
    yl, c = section // 2, lax.rem(section, 2)
    y = yh * nyl + yl

    def at(x_to, z_to, y_to, c_to):
        return (lax.rem(y_to, nyl) * 2 + c_to, x_to * nz + z_to, y_to // nyl)

    def ring(value, size):
        return lax.rem(value + 2 * size, size)

    twin = at(x, z, y, 1 - c)
    above, below = at(x, ring(z + 1, nz), y, c), at(x, ring(z - 1, nz), y, c)
    across = at(x, z, ring(y + nyl, ny), c)
    pair = at(x, z, (1 - yh) * nyl + (nyl - 1 - yl), c)

    numbers = {}
    started = []

    def number_of(name):
        return numbers.setdefault(name, len(numbers))

    def copy(name, src, dst, to):
        number = number_of(name)
        return pltpu.make_async_remote_copy(
            src_ref=src, dst_ref=dst, send_sem=send_sem.at[number], recv_sem=recv_sem.at[number],
            device_id=to, device_id_type=MESH,
        )

    def go(name, src, dst, to):
        one = copy(name, src, dst, to)
        one.start()
        started.append(one)

    def arrived(name, dst):
        copy(name, dst, dst, twin).wait_recv()

    loads = []
    for h in range(2):
        for i, ref in enumerate((w_gate, w_up, w_down)):
            load = pltpu.make_async_copy(
                ref.at[pl.ds(h * feats, feats), :], weights.at[h, :, pl.ds(i * hid, hid)], load_sem.at[3 * h + i]
            )
            load.start()
            loads.append(load)
    barrier = pltpu.get_barrier_semaphore()
    for step in range(1, 2 * ny):
        other = ring(y * 2 + c + step, 2 * ny)
        pl.semaphore_signal(barrier, inc=1, device_id=at(x, z, other // 2, lax.rem(other, 2)), device_id_type=MESH)
    for step in range(1, nx):
        pl.semaphore_signal(barrier, inc=1, device_id=at(ring(x + step, nx), z, y, c), device_id_type=MESH)
    pl.semaphore_signal(barrier, inc=1, device_id=above, device_id_type=MESH)
    pl.semaphore_signal(barrier, inc=1, device_id=below, device_id_type=MESH)

    row = lax.broadcasted_iota(jnp.int32, (128, td), 0)
    gates = jnp.zeros((128, td), F32)
    for k in range(2):
        gates = gates + jnp.where(expert_ids[k : k + 1, :] == row, gate_probs[k : k + 1, :], 0.0)
    share[yh] = gates.T
    other_half = pl.ds(pl.multiple_of((1 - yh) * 2 * feats + c * feats, 128), feats)
    own_half = pl.ds(pl.multiple_of(yh * 2 * feats + c * feats, 128), feats)
    staged[0] = tok[:, other_half]
    staged[1] = grd[:, other_half]
    xs[yh, 0] = tok[:, own_half]
    xs[yh, 1] = grd[:, own_half]
    pl.semaphore_wait(barrier, 2 * ny - 1 + nx - 1 + 2)
    go("share", share.at[yh], share.at[yh], pair)
    go("pair", staged, xs.at[yh], pair)

    before = lax.broadcasted_iota(jnp.int32, (td, td), 1) < lax.broadcasted_iota(jnp.int32, (td, td), 0)
    before = jnp.where(before, 1.0, 0.0).astype(BF16)
    slot = lax.broadcasted_iota(jnp.int32, (2 * td, slots), 1).astype(F32)
    shift = jnp.where(lax.broadcasted_iota(jnp.int32, (2 * td, 1), 0) < td, 0.0, 2.0 * CAP)

    def tables(d):
        gate = share[d]
        first = (d * CAP).astype(F32)
        chosen = jnp.where(gate > 0.0, 1.0, 0.0)
        rank = jnp.dot(before, chosen.astype(BF16), preferred_element_type=F32)
        ones = jnp.ones((td, 128), F32)
        for e in range(nx):
            rank_e, chosen_e = rank[:, e : e + 1], chosen[:, e : e + 1]
            rank2 = jnp.concatenate([rank_e, rank_e], axis=0) + (shift + first)
            chosen2 = jnp.concatenate([chosen_e, chosen_e], axis=0)
            picks[e, d] = (jnp.where(rank2 == slot, 1.0, 0.0) * chosen2).astype(BF16)
            gate_e = jnp.broadcast_to(gate[:, e : e + 1], (td, 128))
            scales[e, d] = jnp.concatenate([ones, gate_e], axis=0)

    tables(yh)
    arrived("share", share.at[1 - yh])
    tables(1 - yh)
    arrived("pair", xs.at[1 - yh])
    stacked = xs[...].reshape(4 * td, feats).astype(F32)

    def pick_for(e):
        scale = scales[e].reshape(4 * td, 128)[:, :1]
        rows = (scale * stacked).astype(BF16)
        return rows_dot(picks[e].reshape(4 * td, slots), rows).astype(BF16)

    def first_of(k):
        return 0 if k == 0 else 2 * k - 1

    def size_of(k):
        return 1 if k in (0, half) else 2

    def span(k):
        return pl.ds(first_of(k), size_of(k))

    def landing(k, side):
        return nz - 1 if k == half else 2 * k - 1 + side

    def sends(t, k, p, side):
        return k < half or p == side

    width = feats // 2

    def column(i):
        return slice(i * width, (i + 1) * width)

    def columns_of(ref, i):
        return ref.at[:, pl.ds(i * width, width)]

    def gather_start(j):
        t, p = j // 2, j % 2
        for i in range(2):
            part = columns_of(gathered.at[c, t, 0, p], i)
            if j:
                arrived(("expert", j, i), part)
            for side, to in ((0, above), (1, below)):
                if sends(t, 1, p, side):
                    go(("gather", t, 1, p, i, side), part, columns_of(gathered.at[c, t, landing(1, side), p], i), to)

    def gather_take(t, k):
        for p in range(2):
            for i in range(2):
                for side, to in ((0, above), (1, below)):
                    if sends(t, k, p, side):
                        part = columns_of(gathered.at[c, t, landing(k, side), p], i)
                        arrived(("gather", t, k, p, i, side), part)
                        if k < half and sends(t, k + 1, p, side):
                            there = columns_of(gathered.at[c, t, landing(k + 1, side), p], i)
                            go(("gather", t, k + 1, p, i, side), part, there, to)
        twin_share(t, k)

    def twin_share(t, k):
        part = gathered.at[c, t, span(k)]
        go(("twin", t, k), part, part, twin)

    def compute_h(t, k):
        arrived(("twin", t, k), gathered.at[1 - c, t, span(k)])
        n, first = size_of(k), first_of(k)
        total = jnp.dot(
            gathered[0, t, first : first + n].reshape(n * 2 * slots, feats), weights[0], preferred_element_type=F32
        ) + jnp.dot(
            gathered[1, t, first : first + n].reshape(n * 2 * slots, feats), weights[1], preferred_element_type=F32
        )
        total = total.reshape(n * 2, slots, 3 * hid)
        value = jnp.concatenate([total[:, :near, : 2 * hid], total[:, near:, 2 * hid :]], axis=2)
        value = value.reshape(n, slots, 3 * hid)
        h_own[t, first : first + n] = value
        h_send[t, first : first + n] = value.astype(BF16)
        for b in range(first, first + n):
            go(("swap", t, b), h_send.at[t, b], h_other.at[t, b], across)

    def outputs(t, k):
        n, first = size_of(k), first_of(k)
        for b in range(first, first + n):
            arrived(("swap", t, b), h_other.at[t, b])
        full = h_own[t, first : first + n] + h_other[t, first : first + n].astype(F32)
        full = full.reshape(n * slots, 3 * hid)
        gate_pre, up_pre, act_grad = full[:, :hid], full[:, hid : 2 * hid], full[:, 2 * hid :]
        sigmoid_gate = jax.nn.sigmoid(gate_pre)
        silu = gate_pre * sigmoid_gate
        activation = silu * up_pre
        up_grad = act_grad * silu
        gate_grad = act_grad * up_pre * sigmoid_gate * (1.0 + gate_pre * (1.0 - sigmoid_gate))
        zero = jnp.zeros_like(activation)
        upper = jnp.concatenate([gate_grad, up_grad, zero], axis=1).reshape(n * 2, near, 3 * hid)
        lower = jnp.concatenate([zero, zero, activation], axis=1).reshape(n * 2, near, 3 * hid)
        value = jnp.concatenate([upper, lower], axis=1).reshape(n * 2 * slots, 3 * hid).astype(BF16)
        hidden[t, first : first + n] = value.reshape(n, 2, slots, 3 * hid)
        o_send[t, first : first + n] = cols_dot(value, weights[1 - c]).astype(BF16).reshape(n, 2, slots, feats)
        go(("out", t, k), o_send.at[t, span(k)], o_twin.at[t, span(k)], twin)
        o_own[t, first : first + n] = cols_dot(value, weights[c]).reshape(n, 2, slots, feats)

    def own_sum(t, b, p, i):
        return o_own[t, b, p, :, column(i)] + o_twin[t, b, p, :, column(i)].astype(F32)

    def sum_step(t, step):
        away = half + 1 - step
        arrived(("out", t, away), o_twin.at[t, span(away)])
        parts = [(p, i, side) for p in range(2) for i in range(2) for side in range(2)]
        if step == 1:
            parts = [part for part in parts if part[0] == part[2]]
        if step == 2:
            parts.sort(key=lambda part: part[0] == part[2])
        for p, i, side in parts:
            to, out_ref, in_ref = ((above, up_send, up_recv), (below, down_send, down_recv))[side]
            value = own_sum(t, nz - 1 if step == 1 else 2 * away - side, p, i)
            if step > 2 or (step == 2 and p == side):
                arrived(("sum", t, step - 1, p, i, side), columns_of(in_ref.at[t, step - 1, p], i))
                value = value + in_ref[t, step - 1, p, :, column(i)].astype(F32)
            out_ref[t, step, p, :, column(i)] = value.astype(BF16)
            go(
                ("sum", t, step, p, i, side),
                columns_of(out_ref.at[t, step, p], i), columns_of(in_ref.at[t, step, p], i), to,
            )

    def sum_end(t):
        arrived(("out", t, 0), o_twin.at[t, span(0)])
        for p in range(2):
            j = 2 * t + p
            for i in range(2):
                for side, in_ref in ((0, up_recv), (1, down_recv)):
                    arrived(("sum", t, half, p, i, side), columns_of(in_ref.at[t, half, p], i))
                value = own_sum(t, 0, p, i) + up_recv[t, half, p, :, column(i)].astype(F32)
                value = value + down_recv[t, half, p, :, column(i)].astype(F32)
                if j:
                    back_send[t, p, :, column(i)] = value.astype(BF16)
                else:
                    back_recv[0, :, column(i)] = value.astype(BF16)
            if j:
                go(("back", j), back_send.at[t, p], back_recv.at[j], at(ring(x - j, nx), z, y, c))

    def combine(t):
        total = jnp.zeros((4 * td, feats), F32)
        for j in (2 * t, 2 * t + 1):
            if j:
                arrived(("back", j), back_recv.at[j])
            e = ring(x + j, nx)
            scale = scales[e].reshape(4 * td, 128)[:, :1]
            total = total + scale * jnp.dot(
                picks[e].reshape(4 * td, slots), back_recv[j], preferred_element_type=F32
            )
        return total

    tile = min(feats, 256)
    tiles = 2 * (feats // tile)

    def weight_grads(first, last):
        def turn(i, carry):
            h, j = i // (feats // tile), lax.rem(i, feats // tile)
            left = gathered[h, :, :, :, :, pl.ds(pl.multiple_of(j * tile, 128), tile)]
            value = rows_dot(
                left.reshape(nz * nx * slots, tile), hidden[...].reshape(nz * nx * slots, 3 * hid)
            ).astype(BF16)
            rows = pl.ds(pl.multiple_of(i * tile, 128), tile)
            for part in range(3):
                grads[part, rows, :] = value[:, part * hid : (part + 1) * hid]
            return carry
        lax.fori_loop(first, last, turn, 0)

    gathered[c, 0, 0, 0] = pick_for(x)
    gather_start(0)
    for j in sorted(range(1, nx), key=lambda j: min(j, nx - j)):
        e = ring(x + j, nx)
        rsend[j] = pick_for(e)
        for i in range(2):
            part = columns_of(gathered.at[c, j // 2, 0, j % 2], i)
            go(("expert", j, i), columns_of(rsend.at[j], i), part, at(e, z, y, c))
    gather_start(1)
    twin_share(0, 0)

    def enter():
        for j in (3, 2):
            gather_start(j)
        twin_share(1, 0)

    def valid(k):
        return 0 <= k <= half

    for turn in range(1, half + LAG + 1):
        if turn <= half:
            gather_take(0, turn)
        if turn == LAG:
            enter()
        if turn == 1:
            for load in loads:
                load.wait()
        if turn <= half:
            compute_h(0, turn - 1)
        if turn > LAG:
            gather_take(1, turn - LAG)
        if valid(turn - LAG - 1):
            compute_h(1, turn - LAG - 1)
        if turn == half:
            compute_h(0, half)
        if valid(turn - 3) and turn < half + LAG:
            outputs(0, turn - 3)
    compute_h(1, half)
    outputs(0, half)
    for k in range(half + LAG - 3, half):
        outputs(0, k)
    sum_step(0, 1)
    outputs(1, 0)
    if half > 2:
        sum_step(0, 2)
    for k in range(1, half + 1):
        outputs(1, k)
    for step in range(3, half):
        sum_step(0, step)
    sum_step(1, 1)
    weight_grads(0, tiles // 6)
    sum_step(0, half)
    sum_step(1, 2)
    weight_grads(tiles // 6, tiles // 2)
    sum_end(0)
    for step in range(3, half):
        sum_step(1, step)
    weight_grads(tiles // 2, 5 * tiles // 6)
    if half > 2:
        sum_step(1, half)
    weight_grads(5 * tiles // 6, tiles)
    results = []
    for i, ref in enumerate((d_gate, d_up, d_down)):
        result = pltpu.make_async_copy(grads.at[i], ref, load_sem.at[6 + i])
        result.start()
        results.append(result)
    combined = combine(0)
    sum_end(1)
    combined = (combined + combine(1)).astype(BF16)
    share_of = feats // nq
    for d in range(2):
        for q in range(nq):
            last_send[d, q] = combined[2 * d * td : 2 * (d + 1) * td, q * share_of : (q + 1) * share_of]
    copies = []
    senders = [number_of(("last", i)) for i in range(2 * nq)]
    takers = [number_of(("take", i)) for i in range(nyl)]
    for d in range(2):
        for q in range(nq):
            owner = yh * nyl + c * nq + q
            y_to, c_to = d * nyl + owner // 2, lax.rem(owner, 2)
            mine = jnp.logical_and(y_to == y, c_to == c)
            one = pltpu.make_async_remote_copy(
                src_ref=last_send.at[d, q], dst_ref=last_recv.at[yl],
                send_sem=send_sem.at[senders[d * nq + q]], recv_sem=recv_sem.at[takers[0] + yl],
                device_id=at(x, z, y_to, c_to), device_id_type=MESH,
            )
            copies.append((mine, one))

            @pl.when(mine)
            def _():
                last_recv[yl] = last_send[d, q]

            @pl.when(jnp.logical_not(mine))
            def _():
                one.start()

    from_yh, from_c = section // nyl, lax.rem(section, nyl) // nq
    for yl_from in range(nyl):
        mine = jnp.logical_and(from_yh * nyl + yl_from == y, from_c == c)

        @pl.when(jnp.logical_not(mine))
        def _():
            arrived(("take", yl_from), last_recv.at[yl_from])

    total = last_recv[0].astype(F32)
    for yl_from in range(1, nyl):
        total = total + last_recv[yl_from].astype(F32)
    gin[...] = total[:td].astype(BF16)
    moe[...] = total[td:].astype(BF16)

    for one in results:
        one.wait()
    for one in started:
        one.wait_send()
    for mine, one in copies:

        @pl.when(jnp.logical_not(mine))
        def _():
            one.wait_send()


SEMAPHORES = 192


def local(nyl, tokens, grad_out, expert_ids, gate_probs, gate_weight, up_weight, down_weight):
    td, width = tokens.shape
    hid = gate_weight.shape[1]
    nx = EXP
    nz = lax.axis_size("expert") // nx
    feats = width // 4
    nq = nyl // 2
    slots = 4 * CAP
    half = nz // 2
    vmem = pl.BlockSpec(memory_space=pltpu.VMEM)
    out_token = jax.ShapeDtypeStruct((td, width // (2 * nyl)), BF16)
    out_weight = jax.ShapeDtypeStruct(gate_weight.shape, BF16)
    exchange = pltpu.VMEM((2, nz, slots, 3 * hid), BF16)
    outs = pltpu.VMEM((2, nz, 2, slots, feats), BF16)
    ring_slots = pltpu.VMEM((2, half + 1, 2, slots, feats), BF16)
    anywhere = pl.BlockSpec(memory_space=pl.ANY)
    results = pl.pallas_call(
        functools.partial(kernel, (nx, nz, nyl, feats, hid, td)),
        out_shape=(out_token, out_token, out_weight, out_weight, out_weight),
        in_specs=[vmem] * 4 + [anywhere] * 3,
        out_specs=(vmem,) * 2 + (anywhere,) * 3,
        scratch_shapes=[
            pltpu.VMEM((2, td, feats), BF16),
            pltpu.VMEM((2, 2, td, feats), BF16),
            pltpu.VMEM((2, td, 128), F32),
            pltpu.VMEM((nx, 2, 2 * td, slots), BF16),
            pltpu.VMEM((nx, 2, 2 * td, 128), F32),
            pltpu.VMEM((nx, slots, feats), BF16),
            pltpu.VMEM((2, 2, nz, 2, slots, feats), BF16),
            pltpu.VMEM((2, feats, 3 * hid), BF16),
            pltpu.VMEM((2, nz, slots, 3 * hid), F32),
            exchange,
            exchange,
            pltpu.VMEM((2, nz, 2, slots, 3 * hid), BF16),
            pltpu.VMEM((2, nz, 2, slots, feats), F32),
            outs,
            outs,
            ring_slots,
            ring_slots,
            ring_slots,
            ring_slots,
            pltpu.VMEM((2, 2, slots, feats), BF16),
            pltpu.VMEM((nx, slots, feats), BF16),
            pltpu.VMEM((2, nq, 2 * td, feats // nq), BF16),
            pltpu.VMEM((nyl, 2 * td, feats // nq), BF16),
            pltpu.VMEM((3, 2 * feats, hid), BF16),
            pltpu.SemaphoreType.DMA((SEMAPHORES,)),
            pltpu.SemaphoreType.DMA((SEMAPHORES,)),
            pltpu.SemaphoreType.DMA((9,)),
        ],
        compiler_params=pltpu.CompilerParams(
            collective_id=0, has_side_effects=True, vmem_limit_bytes=60 * 1024 * 1024
        ),
        name="moe_layer",
    )(tokens, grad_out, expert_ids.T, gate_probs.T, gate_weight, up_weight, down_weight)
    return pl.pallas_call(
        hand_on,
        out_shape=tuple(jax.ShapeDtypeStruct(one.shape, one.dtype) for one in results),
        in_specs=[vmem] * 5,
        out_specs=(vmem,) * 5,
        name="hand_on",
    )(*results)


def hand_on(*refs):
    for source, target in zip(refs[:5], refs[5:]):
        target[...] = source[...]


def solution(mesh):
    return jax.shard_map(
        functools.partial(local, mesh.shape["section"] // 2),
        mesh=mesh,
        in_specs=(
            P(("expert", "dp"), None),
            P(("expert", "dp"), None),
            P(("expert", "dp"), None),
            P(("expert", "dp"), None),
            P("dp", ("expert", "section")),
            P("dp", ("expert", "section")),
            P("dp", ("expert", "section")),
        ),
        out_specs=(
            P(("expert", "dp"), "section"),
            P(("expert", "dp"), "section"),
            P("dp", ("expert", "section")),
            P("dp", ("expert", "section")),
            P("dp", ("expert", "section")),
        ),
        check_vma=False,
    )
```

```python
import functools

import jax
import jax.numpy as jnp
from jax import lax
from jax.experimental import pallas as pl
from jax.experimental.pallas import tpu as pltpu
from jax.sharding import PartitionSpec as P

EXP = 4
CAP = 12
MESH = pl.DeviceIdType.MESH
F32 = jnp.float32
BF16 = jnp.bfloat16


def rows_dot(left, right):
    return lax.dot_general(left, right, (((0,), (0,)), ((), ())), preferred_element_type=F32)


def cols_dot(left, right):
    return lax.dot_general(left, right, (((1,), (1,)), ((), ())), preferred_element_type=F32)


LAG = 2


def kernel(
    dims,
    tok, grd, expert_ids, gate_probs, w_gate, w_up, w_down,
    moe, gin, d_gate, d_up, d_down,
    staged, xs, share, picks, scales, rsend, gathered, weights,
    h_own, h_send, h_other, hidden,
    o_own, o_send, o_twin, up_send, down_send, up_recv, down_recv,
    back_send, back_recv, last_send, last_recv, grads, send_sem, recv_sem, load_sem,
):
    nx, nz, nyl, feats, hid, td = dims
    half, nq = nz // 2, nyl // 2
    ny = 2 * nyl
    slots = 4 * CAP
    near = slots // 2
    section, place, yh = lax.axis_index("section"), lax.axis_index("expert"), lax.axis_index("dp")
    x, z = place // nz, lax.rem(place, nz)
    yl, c = section // 2, lax.rem(section, 2)
    y = yh * nyl + yl

    def at(x_to, z_to, y_to, c_to):
        return (lax.rem(y_to, nyl) * 2 + c_to, x_to * nz + z_to, y_to // nyl)

    def ring(value, size):
        return lax.rem(value + 2 * size, size)

    twin = at(x, z, y, 1 - c)
    above, below = at(x, ring(z + 1, nz), y, c), at(x, ring(z - 1, nz), y, c)
    across = at(x, z, ring(y + nyl, ny), c)
    pair = at(x, z, (1 - yh) * nyl + (nyl - 1 - yl), c)

    numbers = {}
    started = []

    def number_of(name):
        return numbers.setdefault(name, len(numbers))

    def copy(name, src, dst, to):
        number = number_of(name)
        return pltpu.make_async_remote_copy(
            src_ref=src, dst_ref=dst, send_sem=send_sem.at[number], recv_sem=recv_sem.at[number],
            device_id=to, device_id_type=MESH,
        )

    def go(name, src, dst, to):
        one = copy(name, src, dst, to)
        one.start()
        started.append(one)

    def arrived(name, dst):
        copy(name, dst, dst, twin).wait_recv()

    loads = []
    for h in range(2):
        for i, ref in enumerate((w_gate, w_up, w_down)):
            load = pltpu.make_async_copy(
                ref.at[pl.ds(h * feats, feats), :], weights.at[h, :, pl.ds(i * hid, hid)], load_sem.at[3 * h + i]
            )
            load.start()
            loads.append(load)
    barrier = pltpu.get_barrier_semaphore()
    for step in range(1, 2 * ny):
        other = ring(y * 2 + c + step, 2 * ny)
        pl.semaphore_signal(barrier, inc=1, device_id=at(x, z, other // 2, lax.rem(other, 2)), device_id_type=MESH)
    for step in range(1, nx):
        pl.semaphore_signal(barrier, inc=1, device_id=at(ring(x + step, nx), z, y, c), device_id_type=MESH)
    pl.semaphore_signal(barrier, inc=1, device_id=above, device_id_type=MESH)
    pl.semaphore_signal(barrier, inc=1, device_id=below, device_id_type=MESH)

    row = lax.broadcasted_iota(jnp.int32, (128, td), 0)
    gates = jnp.zeros((128, td), F32)
    for k in range(2):
        gates = gates + jnp.where(expert_ids[k : k + 1, :] == row, gate_probs[k : k + 1, :], 0.0)
    share[yh] = gates.T
    other_half = pl.ds(pl.multiple_of((1 - yh) * 2 * feats + c * feats, 128), feats)
    own_half = pl.ds(pl.multiple_of(yh * 2 * feats + c * feats, 128), feats)
    staged[0] = tok[:, other_half]
    staged[1] = grd[:, other_half]
    xs[yh, 0] = tok[:, own_half]
    xs[yh, 1] = grd[:, own_half]
    pl.semaphore_wait(barrier, 2 * ny - 1 + nx - 1 + 2)
    go("share", share.at[yh], share.at[yh], pair)
    go("pair", staged, xs.at[yh], pair)

    before = lax.broadcasted_iota(jnp.int32, (td, td), 1) < lax.broadcasted_iota(jnp.int32, (td, td), 0)
    before = jnp.where(before, 1.0, 0.0).astype(BF16)
    slot = lax.broadcasted_iota(jnp.int32, (2 * td, slots), 1).astype(F32)
    shift = jnp.where(lax.broadcasted_iota(jnp.int32, (2 * td, 1), 0) < td, 0.0, 2.0 * CAP)

    def tables(d):
        gate = share[d]
        first = (d * CAP).astype(F32)
        chosen = jnp.where(gate > 0.0, 1.0, 0.0)
        rank = jnp.dot(before, chosen.astype(BF16), preferred_element_type=F32)
        ones = jnp.ones((td, 128), F32)
        for e in range(nx):
            rank_e, chosen_e = rank[:, e : e + 1], chosen[:, e : e + 1]
            rank2 = jnp.concatenate([rank_e, rank_e], axis=0) + (shift + first)
            chosen2 = jnp.concatenate([chosen_e, chosen_e], axis=0)
            picks[e, d] = (jnp.where(rank2 == slot, 1.0, 0.0) * chosen2).astype(BF16)
            gate_e = jnp.broadcast_to(gate[:, e : e + 1], (td, 128))
            scales[e, d] = jnp.concatenate([ones, gate_e], axis=0)

    tables(yh)
    arrived("share", share.at[1 - yh])
    tables(1 - yh)
    arrived("pair", xs.at[1 - yh])
    stacked = xs[...].reshape(4 * td, feats).astype(F32)

    def pick_for(e):
        scale = scales[e].reshape(4 * td, 128)[:, :1]
        rows = (scale * stacked).astype(BF16)
        return rows_dot(picks[e].reshape(4 * td, slots), rows).astype(BF16)

    def first_of(k):
        return 0 if k == 0 else 2 * k - 1

    def size_of(k):
        return 1 if k in (0, half) else 2

    def span(k):
        return pl.ds(first_of(k), size_of(k))

    def landing(k, side):
        return nz - 1 if k == half else 2 * k - 1 + side

    def sends(t, k, p, side):
        return k < half or p == side

    width = feats // 2

    def column(i):
        return slice(i * width, (i + 1) * width)

    def columns_of(ref, i):
        return ref.at[:, pl.ds(i * width, width)]

    def gather_start(j):
        t, p = j // 2, j % 2
        for i in range(2):
            part = columns_of(gathered.at[c, t, 0, p], i)
            if j:
                arrived(("expert", j, i), part)
            for side, to in ((0, above), (1, below)):
                if sends(t, 1, p, side):
                    go(("gather", t, 1, p, i, side), part, columns_of(gathered.at[c, t, landing(1, side), p], i), to)

    def gather_take(t, k):
        for p in range(2):
            for i in range(2):
                for side, to in ((0, above), (1, below)):
                    if sends(t, k, p, side):
                        part = columns_of(gathered.at[c, t, landing(k, side), p], i)
                        arrived(("gather", t, k, p, i, side), part)
                        if k < half and sends(t, k + 1, p, side):
                            there = columns_of(gathered.at[c, t, landing(k + 1, side), p], i)
                            go(("gather", t, k + 1, p, i, side), part, there, to)
        twin_share(t, k)

    def twin_share(t, k):
        part = gathered.at[c, t, span(k)]
        go(("twin", t, k), part, part, twin)

    def compute_h(t, k):
        arrived(("twin", t, k), gathered.at[1 - c, t, span(k)])
        n, first = size_of(k), first_of(k)
        total = jnp.dot(
            gathered[0, t, first : first + n].reshape(n * 2 * slots, feats), weights[0], preferred_element_type=F32
        ) + jnp.dot(
            gathered[1, t, first : first + n].reshape(n * 2 * slots, feats), weights[1], preferred_element_type=F32
        )
        total = total.reshape(n * 2, slots, 3 * hid)
        value = jnp.concatenate([total[:, :near, : 2 * hid], total[:, near:, 2 * hid :]], axis=2)
        value = value.reshape(n, slots, 3 * hid)
        h_own[t, first : first + n] = value
        h_send[t, first : first + n] = value.astype(BF16)
        for b in range(first, first + n):
            go(("swap", t, b), h_send.at[t, b], h_other.at[t, b], across)

    def outputs(t, k):
        n, first = size_of(k), first_of(k)
        for b in range(first, first + n):
            arrived(("swap", t, b), h_other.at[t, b])
        full = h_own[t, first : first + n] + h_other[t, first : first + n].astype(F32)
        full = full.reshape(n * slots, 3 * hid)
        gate_pre, up_pre, act_grad = full[:, :hid], full[:, hid : 2 * hid], full[:, 2 * hid :]
        sigmoid_gate = jax.nn.sigmoid(gate_pre)
        silu = gate_pre * sigmoid_gate
        activation = silu * up_pre
        up_grad = act_grad * silu
        gate_grad = act_grad * up_pre * sigmoid_gate * (1.0 + gate_pre * (1.0 - sigmoid_gate))
        zero = jnp.zeros_like(activation)
        upper = jnp.concatenate([gate_grad, up_grad, zero], axis=1).reshape(n * 2, near, 3 * hid)
        lower = jnp.concatenate([zero, zero, activation], axis=1).reshape(n * 2, near, 3 * hid)
        value = jnp.concatenate([upper, lower], axis=1).reshape(n * 2 * slots, 3 * hid).astype(BF16)
        hidden[t, first : first + n] = value.reshape(n, 2, slots, 3 * hid)
        o_send[t, first : first + n] = cols_dot(value, weights[1 - c]).astype(BF16).reshape(n, 2, slots, feats)
        go(("out", t, k), o_send.at[t, span(k)], o_twin.at[t, span(k)], twin)
        o_own[t, first : first + n] = cols_dot(value, weights[c]).reshape(n, 2, slots, feats)

    def own_sum(t, b, p, i):
        return o_own[t, b, p, :, column(i)] + o_twin[t, b, p, :, column(i)].astype(F32)

    def sum_step(t, step):
        away = half + 1 - step
        arrived(("out", t, away), o_twin.at[t, span(away)])
        parts = [(p, i, side) for p in range(2) for i in range(2) for side in range(2)]
        if step == 1:
            parts = [part for part in parts if part[0] == part[2]]
        if step == 2:
            parts.sort(key=lambda part: part[0] == part[2])
        for p, i, side in parts:
            to, out_ref, in_ref = ((above, up_send, up_recv), (below, down_send, down_recv))[side]
            value = own_sum(t, nz - 1 if step == 1 else 2 * away - side, p, i)
            if step > 2 or (step == 2 and p == side):
                arrived(("sum", t, step - 1, p, i, side), columns_of(in_ref.at[t, step - 1, p], i))
                value = value + in_ref[t, step - 1, p, :, column(i)].astype(F32)
            out_ref[t, step, p, :, column(i)] = value.astype(BF16)
            go(
                ("sum", t, step, p, i, side),
                columns_of(out_ref.at[t, step, p], i), columns_of(in_ref.at[t, step, p], i), to,
            )

    def sum_end(t):
        arrived(("out", t, 0), o_twin.at[t, span(0)])
        for p in range(2):
            j = 2 * t + p
            for i in range(2):
                for side, in_ref in ((0, up_recv), (1, down_recv)):
                    arrived(("sum", t, half, p, i, side), columns_of(in_ref.at[t, half, p], i))
                value = own_sum(t, 0, p, i) + up_recv[t, half, p, :, column(i)].astype(F32)
                value = value + down_recv[t, half, p, :, column(i)].astype(F32)
                if j:
                    back_send[t, p, :, column(i)] = value.astype(BF16)
                else:
                    back_recv[0, :, column(i)] = value.astype(BF16)
            if j:
                go(("back", j), back_send.at[t, p], back_recv.at[j], at(ring(x - j, nx), z, y, c))

    def combine(t):
        total = jnp.zeros((4 * td, feats), F32)
        for j in (2 * t, 2 * t + 1):
            if j:
                arrived(("back", j), back_recv.at[j])
            e = ring(x + j, nx)
            scale = scales[e].reshape(4 * td, 128)[:, :1]
            total = total + scale * jnp.dot(
                picks[e].reshape(4 * td, slots), back_recv[j], preferred_element_type=F32
            )
        return total

    tile = min(feats, 256)
    tiles = 2 * (feats // tile)

    def weight_grads(first, last):
        def turn(i, carry):
            h, j = i // (feats // tile), lax.rem(i, feats // tile)
            left = gathered[h, :, :, :, :, pl.ds(pl.multiple_of(j * tile, 128), tile)]
            value = rows_dot(
                left.reshape(nz * nx * slots, tile), hidden[...].reshape(nz * nx * slots, 3 * hid)
            ).astype(BF16)
            rows = pl.ds(pl.multiple_of(i * tile, 128), tile)
            for part in range(3):
                grads[part, rows, :] = value[:, part * hid : (part + 1) * hid]
            return carry
        lax.fori_loop(first, last, turn, 0)

    gathered[c, 0, 0, 0] = pick_for(x)
    gather_start(0)
    for j in sorted(range(1, nx), key=lambda j: min(j, nx - j)):
        e = ring(x + j, nx)
        rsend[j] = pick_for(e)
        for i in range(2):
            part = columns_of(gathered.at[c, j // 2, 0, j % 2], i)
            go(("expert", j, i), columns_of(rsend.at[j], i), part, at(e, z, y, c))
    gather_start(1)
    twin_share(0, 0)

    def enter():
        for j in (3, 2):
            gather_start(j)
        twin_share(1, 0)

    def valid(k):
        return 0 <= k <= half

    for turn in range(1, half + LAG + 1):
        if turn <= half:
            gather_take(0, turn)
        if turn == LAG:
            enter()
        if turn == 1:
            for load in loads:
                load.wait()
        if turn <= half:
            compute_h(0, turn - 1)
        if turn > LAG:
            gather_take(1, turn - LAG)
        if valid(turn - LAG - 1):
            compute_h(1, turn - LAG - 1)
        if turn == half:
            compute_h(0, half)
        if valid(turn - 3) and turn < half + LAG:
            outputs(0, turn - 3)
    compute_h(1, half)
    outputs(0, half)
    for k in range(half + LAG - 3, half):
        outputs(0, k)
    sum_step(0, 1)
    outputs(1, 0)
    if half > 2:
        sum_step(0, 2)
    for k in range(1, half + 1):
        outputs(1, k)
    for step in range(3, half):
        sum_step(0, step)
    sum_step(1, 1)
    weight_grads(0, tiles // 6)
    sum_step(0, half)
    sum_step(1, 2)
    weight_grads(tiles // 6, tiles // 2)
    sum_end(0)
    for step in range(3, half):
        sum_step(1, step)
    weight_grads(tiles // 2, 5 * tiles // 6)
    if half > 2:
        sum_step(1, half)
    weight_grads(5 * tiles // 6, tiles)
    results = []
    for i, ref in enumerate((d_gate, d_up, d_down)):
        result = pltpu.make_async_copy(grads.at[i], ref, load_sem.at[6 + i])
        result.start()
        results.append(result)
    combined = combine(0)
    sum_end(1)
    combined = (combined + combine(1)).astype(BF16)
    share_of = feats // nq
    for d in range(2):
        for q in range(nq):
            last_send[d, q] = combined[2 * d * td : 2 * (d + 1) * td, q * share_of : (q + 1) * share_of]
    copies = []
    senders = [number_of(("last", i)) for i in range(2 * nq)]
    takers = [number_of(("take", i)) for i in range(nyl)]
    for d in range(2):
        for q in range(nq):
            owner = yh * nyl + c * nq + q
            y_to, c_to = d * nyl + owner // 2, lax.rem(owner, 2)
            mine = jnp.logical_and(y_to == y, c_to == c)
            one = pltpu.make_async_remote_copy(
                src_ref=last_send.at[d, q], dst_ref=last_recv.at[yl],
                send_sem=send_sem.at[senders[d * nq + q]], recv_sem=recv_sem.at[takers[0] + yl],
                device_id=at(x, z, y_to, c_to), device_id_type=MESH,
            )
            copies.append((mine, one))

            @pl.when(mine)
            def _():
                last_recv[yl] = last_send[d, q]

            @pl.when(jnp.logical_not(mine))
            def _():
                one.start()

    from_yh, from_c = section // nyl, lax.rem(section, nyl) // nq
    for yl_from in range(nyl):
        mine = jnp.logical_and(from_yh * nyl + yl_from == y, from_c == c)

        @pl.when(jnp.logical_not(mine))
        def _():
            arrived(("take", yl_from), last_recv.at[yl_from])

    total = last_recv[0].astype(F32)
    for yl_from in range(1, nyl):
        total = total + last_recv[yl_from].astype(F32)
    gin[...] = total[:td].astype(BF16)
    moe[...] = total[td:].astype(BF16)

    for one in results:
        one.wait()
    for one in started:
        one.wait_send()
    for mine, one in copies:

        @pl.when(jnp.logical_not(mine))
        def _():
            one.wait_send()


SEMAPHORES = 192


def local(nyl, tokens, grad_out, expert_ids, gate_probs, gate_weight, up_weight, down_weight):
    td, width = tokens.shape
    hid = gate_weight.shape[1]
    nx = EXP
    nz = lax.axis_size("expert") // nx
    feats = width // 4
    nq = nyl // 2
    slots = 4 * CAP
    half = nz // 2
    vmem = pl.BlockSpec(memory_space=pltpu.VMEM)
    out_token = jax.ShapeDtypeStruct((td, width // (2 * nyl)), BF16)
    out_weight = jax.ShapeDtypeStruct(gate_weight.shape, BF16)
    exchange = pltpu.VMEM((2, nz, slots, 3 * hid), BF16)
    outs = pltpu.VMEM((2, nz, 2, slots, feats), BF16)
    ring_slots = pltpu.VMEM((2, half + 1, 2, slots, feats), BF16)
    anywhere = pl.BlockSpec(memory_space=pl.ANY)
    results = pl.pallas_call(
        functools.partial(kernel, (nx, nz, nyl, feats, hid, td)),
        out_shape=(out_token, out_token, out_weight, out_weight, out_weight),
        in_specs=[vmem] * 4 + [anywhere] * 3,
        out_specs=(vmem,) * 2 + (anywhere,) * 3,
        scratch_shapes=[
            pltpu.VMEM((2, td, feats), BF16),
            pltpu.VMEM((2, 2, td, feats), BF16),
            pltpu.VMEM((2, td, 128), F32),
            pltpu.VMEM((nx, 2, 2 * td, slots), BF16),
            pltpu.VMEM((nx, 2, 2 * td, 128), F32),
            pltpu.VMEM((nx, slots, feats), BF16),
            pltpu.VMEM((2, 2, nz, 2, slots, feats), BF16),
            pltpu.VMEM((2, feats, 3 * hid), BF16),
            pltpu.VMEM((2, nz, slots, 3 * hid), F32),
            exchange,
            exchange,
            pltpu.VMEM((2, nz, 2, slots, 3 * hid), BF16),
            pltpu.VMEM((2, nz, 2, slots, feats), F32),
            outs,
            outs,
            ring_slots,
            ring_slots,
            ring_slots,
            ring_slots,
            pltpu.VMEM((2, 2, slots, feats), BF16),
            pltpu.VMEM((nx, slots, feats), BF16),
            pltpu.VMEM((2, nq, 2 * td, feats // nq), BF16),
            pltpu.VMEM((nyl, 2 * td, feats // nq), BF16),
            pltpu.VMEM((3, 2 * feats, hid), BF16),
            pltpu.SemaphoreType.DMA((SEMAPHORES,)),
            pltpu.SemaphoreType.DMA((SEMAPHORES,)),
            pltpu.SemaphoreType.DMA((9,)),
        ],
        compiler_params=pltpu.CompilerParams(
            collective_id=0, has_side_effects=True, vmem_limit_bytes=60 * 1024 * 1024
        ),
        name="moe_layer",
    )(tokens, grad_out, expert_ids.T, gate_probs.T, gate_weight, up_weight, down_weight)
    return pl.pallas_call(
        hand_on,
        out_shape=tuple(jax.ShapeDtypeStruct(one.shape, one.dtype) for one in results),
        in_specs=[anywhere] * 5,
        out_specs=(anywhere,) * 5,
        scratch_shapes=[pltpu.VMEM(one.shape, one.dtype) for one in results] + [pltpu.SemaphoreType.DMA((10,))],
        name="hand_on",
    )(*results)


def hand_on(*refs):
    sem = refs[15]
    taken = [pltpu.make_async_copy(refs[i], refs[10 + i], sem.at[i]) for i in range(5)]
    given = [pltpu.make_async_copy(refs[10 + i], refs[5 + i], sem.at[5 + i]) for i in range(5)]
    for one in taken:
        one.start()
    for one, other in zip(taken, given):
        one.wait()
        other.start()
    for other in given:
        other.wait()


def solution(mesh):
    return jax.shard_map(
        functools.partial(local, mesh.shape["section"] // 2),
        mesh=mesh,
        in_specs=(
            P(("expert", "dp"), None),
            P(("expert", "dp"), None),
            P(("expert", "dp"), None),
            P(("expert", "dp"), None),
            P("dp", ("expert", "section")),
            P("dp", ("expert", "section")),
            P("dp", ("expert", "section")),
        ),
        out_specs=(
            P(("expert", "dp"), "section"),
            P(("expert", "dp"), "section"),
            P("dp", ("expert", "section")),
            P("dp", ("expert", "section")),
            P("dp", ("expert", "section")),
        ),
        check_vma=False,
    )
```
